32 devices in a mesh: dom: 8 (over z, x), tp: 4 (over y, core).
Axes of the slice: x: 2, y: 2, z: 4, core: 2. Of those that a mesh axis runs over, the one named last changes fastest.
Arguments:
- features: bfloat16 [32768, 512], P('dom'), may hold values from -6 to 6
- adjacency: bfloat16 [32768, 128], P('dom'), may hold values from -0.5 to 0.5
- node_mask: int32 [32768], P('dom'), may hold values 0 or 1
- mask_token: bfloat16 [512], replicated, may hold values from -6 to 6
- enc_weight: bfloat16 [512, 512], P(None, 'tp'), may hold values from -0.25 to 0.25
- enc_bias: bfloat16 [512], P('tp'), may hold values from -3 to 3
- gain: float32 [512], replicated, may hold values from -0.25 to 0.25
- requests: int32 [8, 8], P(None, 'dom'), may hold values from 0 to 31
- pair_first: int32 [8, 4, 64], P('dom', 'tp'), may hold values from 0 to 7
- pair_second: int32 [8, 4, 64], P('dom', 'tp'), may hold values from 0 to 9
- label_words: int32 [8, 4, 64, 8, 128], P('dom', 'tp'), may hold values from 0 to 65280
- pair_count: int32 [8, 4], P('dom', 'tp'), may hold values from 16 to 64, as said below
Outputs:
- weight_grad: float32 [512, 512], P(None, 'tp')
- bias_grad: float32 [512], P('tp')
- gain_grad: float32 [512], P('tp')
The draws below stay inside these ranges and needn't reach their ends.
Inputs may be any that keep to these rules, and one draw needn't show every extreme that they name: Every partition requests exactly one block from every partition, itself included. Slots p >= pair_count are padding; some device has all 64 slots live.
All inputs are finite; a program needn't handle non-finite values. No bound on the sum of `node_mask` on one device may be relied on, other than what follows from the above.
Results may differ from the reference program's by a relative error of at most 0.0018.
Values may be sent and summed in bfloat16 or wider, within the bound.
A program may use at most 128 MiB of HBM per device.

```python
import jax
import jax.numpy as jnp
from jax import lax

D = 512
BLK = 128
GROUP = 8
NB_DEV = 32
PAIRS_DEV = 64
NODES = 32768
N_DOM = 8
N_TP = 4


def draw_pair_count(key, part):
    first_key, second_key = jax.random.split(key)
    base = jax.random.randint(first_key, (N_DOM * N_TP,), PAIRS_DEV // 4, PAIRS_DEV + 1)
    where_full = jax.random.randint(second_key, (), 0, N_DOM * N_TP)
    filled = jnp.where(jnp.arange(N_DOM * N_TP) == where_full, PAIRS_DEV, base)
    return filled.reshape(N_DOM, N_TP).astype(jnp.int32)


def plant(array, rng, smallest, largest):
    longest = array.shape.index(max(array.shape))
    spots = []
    for shift in (0, 1):
        where = [jax.random.randint(jax.random.fold_in(rng, axis), (), 0, length) for axis, length in enumerate(array.shape)]
        where[longest] = (where[longest] + shift) % array.shape[longest]
        spots.append(tuple(where))
    return array.at[spots[0]].set(smallest).at[spots[1]].set(largest)


def block_scale(rng, dims, shards, low, high):
    level = 1.0
    for position, parts in shards:
        steps = jax.random.uniform(jax.random.fold_in(jax.random.fold_in(rng, 6), position), (parts,), jnp.float32, low / len(shards), high / len(shards))
        level = level * jnp.repeat(jnp.exp(steps), dims[position] // parts).reshape((-1,) + (1,) * (len(dims) - 1 - position))
    return level


def scatter_about(own_key, shape, spread, bound, cuts=(), kind=jnp.bfloat16):
    drawn = jax.random.normal(own_key, shape, jnp.float32) * spread
    if len(cuts) > 0:
        drawn = block_scale(own_key, shape, cuts, -0.22, 0.18) * drawn
    return jnp.clip(drawn, min=-bound, max=bound).astype(kind)


def setup_inputs(seed: int = 0) -> dict:
    streams_of = jax.random.split(jax.random.key(seed), 13)
    return {
        "features": scatter_about(streams_of[0], (NODES, D), 1.0, 6.0, ((0, 8),)),
        "adjacency": scatter_about(streams_of[1], (NODES, BLK), BLK ** -0.5, 0.5, ((0, 8),)),
        "node_mask": plant((jax.random.randint(streams_of[2], (NODES,), 0, 4) < 1).astype(jnp.int32), jax.random.fold_in(streams_of[2], 1), 0, 1),
        "mask_token": scatter_about(streams_of[3], (D,), 1.0, 6.0),
        "enc_weight": scatter_about(streams_of[4], (D, D), D ** -0.5, 0.25, ((1, 4),)),
        "enc_bias": scatter_about(streams_of[5], (D,), 0.5, 3.0, ((0, 4),)),
        "gain": scatter_about(streams_of[6], (D,), 0.06, 0.25, (), jnp.float32),
        "requests": plant(jax.random.randint(streams_of[7], (N_DOM, N_DOM), 0, NB_DEV), jax.random.fold_in(streams_of[7], 1), 0, NB_DEV - 1).astype(jnp.int32),
        "pair_first": plant(jax.random.randint(streams_of[8], (N_DOM, N_TP, PAIRS_DEV), 0, NB_DEV // N_TP), jax.random.fold_in(streams_of[8], 1), 0, (NB_DEV // N_TP) - 1).astype(jnp.int32),
        "pair_second": plant(jax.random.randint(streams_of[9], (N_DOM, N_TP, PAIRS_DEV), 0, NB_DEV // N_TP + N_DOM // N_TP), jax.random.fold_in(streams_of[9], 1), 0, (NB_DEV // N_TP + N_DOM // N_TP) - 1).astype(jnp.int32),
        "label_words": plant(jax.random.randint(streams_of[10], (N_DOM, N_TP, PAIRS_DEV, BLK // 16, BLK), 0, 65281), jax.random.fold_in(streams_of[10], 1), 0, 65280).astype(jnp.int32),
        "pair_count": draw_pair_count(jax.random.fold_in(streams_of[12], 71), 0),
    }


LOSS_NORM = 256.0


def silu_slope(value):
    sig = jax.nn.sigmoid(value)
    return sig * (1.0 + value * (1.0 - sig))


def unpack_labels(words):
    shifts = jnp.arange(16, dtype=jnp.int32)
    bits = jnp.bitwise_and(jnp.right_shift(words[:, :, None, :], shifts[None, None, :, None]), 1)
    return bits.reshape(words.shape[0], words.shape[1] * 16, words.shape[2]).astype(jnp.float32)


def decode(stack, local_count, first, second, words, count, gain):
    total = stack.shape[0]
    first_acc = jnp.zeros((local_count, stack.shape[1], stack.shape[2]), jnp.float32)
    second_acc = jnp.zeros((total, stack.shape[1], stack.shape[2]), jnp.float32)

    def step(carry, group):
        first_acc, second_acc = carry
        start = group * GROUP
        index_a = lax.dynamic_slice_in_dim(first, start, GROUP, 0)
        index_b = lax.dynamic_slice_in_dim(second, start, GROUP, 0)
        word_rows = lax.dynamic_slice_in_dim(words, start, GROUP, 0)
        tile_a = stack[index_a]
        tile_b = stack[index_b]
        scaled = (tile_a.astype(jnp.float32) * gain[None, None, :]).astype(jnp.bfloat16)
        logits = jnp.einsum("pif,pjf->pij", scaled.astype(jnp.float32), tile_b.astype(jnp.float32))
        live = ((start + jnp.arange(GROUP, dtype=jnp.int32)) < count).astype(jnp.float32)
        slope = ((jax.nn.sigmoid(logits) - unpack_labels(word_rows)) * live[:, None, None] / LOSS_NORM).astype(jnp.bfloat16)
        part_a = jnp.einsum("pij,pjf->pif", slope.astype(jnp.float32), tile_b.astype(jnp.float32))
        part_b = jnp.einsum("pij,pif->pjf", slope.astype(jnp.float32), scaled.astype(jnp.float32))
        return (first_acc.at[index_a].add(part_a), second_acc.at[index_b].add(part_b)), None

    groups = jnp.arange(first.shape[0] // GROUP, dtype=jnp.int32)
    (first_acc, second_acc), _ = lax.scan(step, (first_acc, second_acc), groups)
    return first_acc, second_acc


def reference(features, adjacency, node_mask, mask_token, enc_weight, enc_bias, gain, requests, pair_first, pair_second, label_words, pair_count):
    masked = jnp.where(node_mask[:, None] == 1, mask_token[None, :], features)
    blocks = masked.reshape(-1, BLK, D)
    mixed = jnp.einsum("bij,bjf->bif", adjacency.reshape(-1, BLK, BLK).astype(jnp.float32), blocks.astype(jnp.float32))
    agg = (blocks.astype(jnp.float32) + mixed).reshape(NODES, D).astype(jnp.bfloat16)
    pre = jnp.dot(agg, enc_weight, preferred_element_type=jnp.float32) + enc_bias.astype(jnp.float32)
    z_all = jax.nn.silu(pre).astype(jnp.bfloat16)
    z_blocks = z_all.reshape(N_DOM, NB_DEV, BLK, D)
    own_count = NB_DEV // N_TP
    source_count = N_DOM // N_TP
    grads = jnp.zeros((N_DOM, NB_DEV, BLK, D), jnp.float32)
    gain_total = jnp.zeros((D,), jnp.float32)

    def unit(carry, index):
        grads, gain_total = carry
        part = index // N_TP
        lane = index % N_TP
        mine = lax.dynamic_index_in_dim(z_blocks, part, 0, keepdims=False)
        own_ids = (lane * own_count + jnp.arange(own_count, dtype=jnp.int32)).astype(jnp.int32)
        local = mine[own_ids]
        sources = (lane * source_count + jnp.arange(source_count, dtype=jnp.int32)).astype(jnp.int32)
        wanted = lax.dynamic_index_in_dim(requests, part, 0, keepdims=False)[sources]
        remote = z_blocks[sources, wanted]
        stack = jnp.concatenate([local, remote], axis=0)
        first_acc, second_acc = decode(stack, own_count, pair_first[part, lane], pair_second[part, lane], label_words[part, lane], pair_count[part, lane], gain)
        local_grad = gain[None, None, :] * first_acc + second_acc[:own_count]
        grads = grads.at[part, own_ids].add(local_grad)
        grads = grads.at[sources, wanted].add(second_acc[own_count:])
        gain_total = gain_total + jnp.sum(local.astype(jnp.float32) * first_acc, axis=(0, 1))
        return (grads, gain_total), None

    (grads, gain_total), _ = lax.scan(unit, (grads, gain_total), jnp.arange(N_DOM * N_TP, dtype=jnp.int32))
    dpre = grads.reshape(NODES, D) * silu_slope(pre)
    weight_grad = jnp.dot(agg.T, dpre.astype(jnp.bfloat16), preferred_element_type=jnp.float32)
    bias_grad = jnp.sum(dpre, axis=0)
    return (weight_grad, bias_grad, gain_total)
```

```python
import functools

import jax
import jax.numpy as jnp
from jax import lax
from jax.experimental import pallas as pl
from jax.experimental.pallas import tpu as pltpu
from jax.sharding import PartitionSpec as P

UNROLL = 4
INV_NORM = 1.0 / 256.0
MESH = pl.DeviceIdType.MESH
VMEM_LIMIT = 32 * 1024 * 1024


def sigmoid(value):
    return 0.5 * jnp.tanh(0.5 * value) + 0.5


def vmem():
    return pl.BlockSpec(memory_space=pltpu.VMEM)


def smem():
    return pl.BlockSpec(memory_space=pltpu.SMEM)


def front_kernel(
    own_count, wanted, requests, feat_hbm, adj_hbm, mask, token, weight, bias, gain,
    stack_out, scaled_out, agg_out, slope_out,
    feat, adj, gathered, packed, asked, landed,
    feat_sem, w_send, w_recv, z_send, z_recv,
):
    d = lax.axis_index("dom")
    t = lax.axis_index("tp")
    low = lax.rem(t, 2)
    high = lax.div(t, 2)
    core_peer = high * 2 + (1 - low)
    y_peer = (1 - high) * 2 + low
    a = lax.div(d, wanted)
    j = lax.rem(d, wanted)
    width, quarter = weight.shape
    block = mask.shape[2]

    feat_copy = pltpu.make_async_copy(feat_hbm, feat, feat_sem.at[0])
    adj_copy = pltpu.make_async_copy(adj_hbm, adj, feat_sem.at[1])
    feat_copy.start()
    adj_copy.start()

    barrier = pltpu.get_barrier_semaphore()
    for peer in (core_peer, y_peer):
        pl.semaphore_signal(barrier, inc=1, device_id={"tp": peer}, device_id_type=MESH)

    def pair_of(c):
        return t * wanted + lax.rem(j + c, wanted), a

    for c in range(wanted):
        to_dom, to_tp = pair_of(c)
        back_dom = t * wanted + lax.rem(j - c + wanted, wanted)

        def greet():
            pl.semaphore_signal(barrier, inc=1, device_id=(to_dom, to_tp), device_id_type=MESH)
            pl.semaphore_signal(barrier, inc=1, device_id=(back_dom, to_tp), device_id_type=MESH)

        if c == 0:
            pl.when(a != t)(greet)
        else:
            greet()

    columns = lambda c: pl.ds(pl.multiple_of(c * quarter, quarter), quarter)
    packed[:width, :] = weight[...]
    packed[pl.ds(width, 16), :] = jnp.broadcast_to(bias[...], (16, quarter))
    gathered[:, columns(t)] = packed[...]
    pl.semaphore_wait(barrier, 2 + 2 * wanted - jnp.where(a == t, 2, 0))

    def weight_copy(k, source, column, peer):
        return pltpu.make_async_remote_copy(
            src_ref=source, dst_ref=gathered.at[:, columns(column)],
            send_sem=w_send.at[k], recv_sem=w_recv.at[k],
            device_id={"tp": peer}, device_id_type=MESH,
        )

    across = weight_copy(0, packed, t, y_peer)
    near = weight_copy(1, packed, t, core_peer)
    relay = weight_copy(2, gathered.at[:, columns(y_peer)], y_peer, core_peer)
    across.start()
    near.start()

    rows = lax.broadcasted_iota(jnp.int32, (block, block), 0)
    cols = lax.broadcasted_iota(jnp.int32, (block, block), 1)
    token32 = token[...].astype(jnp.float32)

    def aggregate(node_block, spot):
        hidden = jnp.sum(
            jnp.where(rows == cols, mask[node_block].astype(jnp.float32), 0.0), axis=1, keepdims=True
        )
        masked32 = jnp.where(hidden == 1.0, token32, feat[node_block].astype(jnp.float32))
        mixed = jnp.dot(
            adj[node_block], masked32.astype(jnp.bfloat16), preferred_element_type=jnp.float32
        )
        agg_out[spot] = (masked32 + mixed).astype(jnp.bfloat16)

    feat_copy.wait()
    adj_copy.wait()
    for k in range(wanted):
        aggregate(requests[t * wanted + k], own_count + k)
    across.wait_recv()
    relay.start()
    for k in range(own_count):
        aggregate(t * own_count + k, k)
    near.wait_recv()
    relay.wait_recv()

    matrix = gathered[:width, :]
    shift = gathered[width : width + 1, :].astype(jnp.float32)

    def activate(spot, many):
        agg = agg_out[pl.ds(spot, many)].reshape(many * block, width)
        pre = jnp.dot(agg, matrix, preferred_element_type=jnp.float32) + shift
        sig = sigmoid(pre)
        slope_out[pl.ds(spot, many)] = (sig * (1.0 + pre * (1.0 - sig))).reshape(many, block, width)
        return (pre * sig).astype(jnp.bfloat16).reshape(many, block, width)

    for k in range(wanted):
        asked[k] = activate(own_count + k, 1)[0]

    def z_copy(c):
        return pltpu.make_async_remote_copy(
            src_ref=asked.at[lax.rem(j + c, wanted)], dst_ref=landed.at[j],
            send_sem=z_send.at[c], recv_sem=z_recv.at[c],
            device_id=pair_of(c), device_id_type=MESH,
        )

    pl.when(a != t)(lambda: z_copy(0).start())
    for c in range(1, wanted):
        z_copy(c).start()

    @pl.when(a == t)
    def _():
        landed[j] = asked[j]

    for k in range(0, own_count, 2):
        z = activate(k, 2)
        stack_out[pl.ds(k, 2)] = z
        scaled_out[pl.ds(k, 2)] = (z.astype(jnp.float32) * gain[...][None]).astype(jnp.bfloat16)

    pl.when(a != t)(lambda: z_copy(0).wait())
    for c in range(1, wanted):
        z_copy(c).wait()
    for k in range(wanted):
        stack_out[own_count + k] = landed[k]
    across.wait_send()
    near.wait_send()
    relay.wait_send()


def front(own_count, wanted, requests, feat, adj, mask, token, weight, bias, gain):
    nblocks, block, width = feat.shape
    quarter = weight.shape[1]
    total = own_count + wanted
    dma = pltpu.SemaphoreType.DMA
    anywhere = pl.BlockSpec(memory_space=pltpu.HBM)
    return pl.pallas_call(
        functools.partial(front_kernel, own_count, wanted),
        in_specs=[smem(), anywhere, anywhere] + [vmem()] * 5,
        out_specs=[vmem()] * 4,
        out_shape=(
            jax.ShapeDtypeStruct((total, block, width), jnp.bfloat16),
            jax.ShapeDtypeStruct((own_count, block, width), jnp.bfloat16),
            jax.ShapeDtypeStruct((total, block, width), jnp.bfloat16),
            jax.ShapeDtypeStruct((total, block, width), jnp.float32),
        ),
        scratch_shapes=[
            pltpu.VMEM((nblocks, block, width), jnp.bfloat16),
            pltpu.VMEM((nblocks, block, block), jnp.bfloat16),
            pltpu.VMEM((width + 16, width), jnp.bfloat16),
            pltpu.VMEM((width + 16, quarter), jnp.bfloat16),
            pltpu.VMEM((wanted, block, width), jnp.bfloat16),
            pltpu.VMEM((wanted, block, width), jnp.bfloat16),
            dma((2,)), dma((3,)), dma((3,)), dma((wanted,)), dma((wanted,)),
        ],
        compiler_params=pltpu.CompilerParams(
            collective_id=0, has_side_effects=True, vmem_limit_bytes=VMEM_LIMIT
        ),
    )(requests, feat, adj, mask, token, weight, bias, gain)


def run_pairs(first, second, count, words, stack, scaled, first_acc, second_acc):
    live_count = count[0]
    block = stack.shape[1]
    shifts = lax.broadcasted_iota(jnp.int32, (block // 16, 16, block), 1)

    @pl.loop(0, pl.cdiv(live_count, UNROLL))
    def _(step):
        results = []
        for k in range(UNROLL):
            spot = step * UNROLL + k
            live = spot < live_count
            slot = jnp.where(live, spot, 0)
            ia = first[slot]
            ib = second[slot]
            scaled_a = scaled[ia]
            tile_b = stack[ib]
            logits = lax.dot_general(
                scaled_a, tile_b, (((1,), (1,)), ((), ())), preferred_element_type=jnp.float32
            )
            bits = jnp.bitwise_and(jnp.right_shift(words[slot][:, None, :], shifts), 1)
            label = bits.reshape(block, block).astype(jnp.float32)
            factor = jnp.where(live, INV_NORM, 0.0)
            slope = ((sigmoid(logits) - label) * factor).astype(jnp.bfloat16)
            part_a = jnp.dot(slope, tile_b, preferred_element_type=jnp.float32)
            part_b = lax.dot_general(
                slope, scaled_a, (((0,), (0,)), ((), ())), preferred_element_type=jnp.float32
            )
            results.append((ia, ib, part_a, part_b))
        for ia, ib, part_a, part_b in results:
            first_acc[ia] += part_a
            second_acc[ib] += part_b


def decode_kernel(first, second, count, words, stack, scaled, first_acc, second_out, back_out, second_acc):
    own_count = scaled.shape[0]
    first_acc[...] = jnp.zeros_like(first_acc)
    second_acc[...] = jnp.zeros_like(second_acc)
    run_pairs(first, second, count, words, stack, scaled, first_acc, second_acc)
    second_out[...] = second_acc[:own_count]
    back_out[...] = second_acc[own_count:].astype(jnp.bfloat16)


def decode(first, second, count, words, stack, scaled):
    total, block, width = stack.shape
    own_count = scaled.shape[0]
    return pl.pallas_call(
        decode_kernel,
        in_specs=[smem()] * 3 + [vmem()] * 3,
        out_specs=[vmem()] * 3,
        out_shape=(
            jax.ShapeDtypeStruct((own_count, block, width), jnp.float32),
            jax.ShapeDtypeStruct((own_count, block, width), jnp.float32),
            jax.ShapeDtypeStruct((total - own_count, block, width), jnp.bfloat16),
        ),
        scratch_shapes=[pltpu.VMEM((total, block, width), jnp.float32)],
        compiler_params=pltpu.CompilerParams(vmem_limit_bytes=VMEM_LIMIT),
        cost_estimate=pl.CostEstimate(
            flops=64 * 6 * block * block * width, bytes_accessed=8 << 20, transcendentals=0
        ),
    )(first, second, count, words, stack, scaled)


def reduce_kernel(
    doms, own_count, wanted, first, second, back, stack, agg, slope, gain, weight_out, small_out,
    part, home, dpre, recv_core, sum_core, recv_y, total, recv_dom, recv_small, full,
    core_send, core_recv, y_send, y_recv, dom_send, dom_recv, small_send, small_recv,
    full_send, full_recv, home_send, home_recv,
):
    d = lax.axis_index("dom")
    t = lax.axis_index("tp")
    low = lax.rem(t, 2)
    high = lax.div(t, 2)
    core_peer = high * 2 + (1 - low)
    y_peer = (1 - high) * 2 + low
    width = full.shape[0]
    rows = width // doms

    barrier = pltpu.get_barrier_semaphore()
    for peer in (core_peer, y_peer):
        pl.semaphore_signal(barrier, inc=1, device_id={"tp": peer}, device_id_type=MESH)

    @pl.loop(1, doms)
    def _(o):
        pl.semaphore_signal(
            barrier, inc=1, device_id={"dom": lax.rem(d + o, doms)}, device_id_type=MESH
        )

    a = lax.div(d, wanted)
    j = lax.rem(d, wanted)

    def pair_of(c):
        return t * wanted + lax.rem(j - c + wanted, wanted), a

    for c in range(wanted):
        to_dom, to_tp = pair_of(c)
        from_dom = t * wanted + lax.rem(j + c, wanted)

        def greet():
            pl.semaphore_signal(barrier, inc=1, device_id=(to_dom, to_tp), device_id_type=MESH)
            pl.semaphore_signal(barrier, inc=1, device_id=(from_dom, to_tp), device_id_type=MESH)

        if c == 0:
            pl.when(a != t)(greet)
        else:
            greet()

    pl.semaphore_wait(barrier, doms + 1 + 2 * wanted - jnp.where(a == t, 2, 0))

    def home_copy(c):
        return pltpu.make_async_remote_copy(
            src_ref=back.at[lax.rem(j - c + wanted, wanted)], dst_ref=home.at[j],
            send_sem=home_send.at[c], recv_sem=home_recv.at[c],
            device_id=pair_of(c), device_id_type=MESH,
        )

    pl.when(a != t)(lambda: home_copy(0).start())
    for c in range(1, wanted):
        home_copy(c).start()

    @pl.when(a == t)
    def _():
        home[j] = back[j]

    block = stack.shape[1]
    bias_sum = jnp.zeros((1, width), jnp.float32)
    gain_sum = jnp.zeros((1, width), jnp.float32)
    for k in range(own_count):
        value = first[k]
        gain_sum += jnp.sum(stack[k].astype(jnp.float32) * value, axis=0, keepdims=True)
        value = (gain[...] * value + second[k]) * slope[k]
        bias_sum += jnp.sum(value, axis=0, keepdims=True)
        dpre[pl.ds(k * block, block), :] = value.astype(jnp.bfloat16)

    lanes, _, quarter = part.shape

    def product(start, many, c):
        left = agg[pl.ds(start, many)].reshape(many * block, width)
        right = dpre[pl.ds(start * block, many * block), pl.ds(c * quarter, 2 * quarter)]
        return lax.dot_general(
            left, right, (((0,), (0,)), ((), ())), preferred_element_type=jnp.float32
        )

    for c in range(0, lanes, 2):
        both = product(0, own_count, c)
        for k in range(2):
            part[c + k, :width, :] = both[:, k * quarter : (k + 1) * quarter]

    pl.when(a != t)(lambda: home_copy(0).wait())
    for c in range(1, wanted):
        home_copy(c).wait()
    for k in range(wanted):
        value = home[k].astype(jnp.float32) * slope[own_count + k]
        bias_sum += jnp.sum(value, axis=0, keepdims=True)
        dpre[pl.ds((own_count + k) * block, block), :] = value.astype(jnp.bfloat16)
    for c in range(0, lanes, 2):
        both = product(own_count, wanted, c)
        for k in range(2):
            part[c + k, :width, :] += both[:, k * quarter : (k + 1) * quarter]
    row = lax.broadcasted_iota(jnp.int32, (8, width), 0)
    extra = jnp.where(row == 0, bias_sum, jnp.where(row == 1, gain_sum, 0.0))
    for c in range(lanes):
        part[c, pl.ds(width, 8), :] = extra[:, c * quarter : (c + 1) * quarter]

    def core_copy(h):
        return pltpu.make_async_remote_copy(
            src_ref=part.at[2 * h + 1 - low], dst_ref=recv_core.at[h],
            send_sem=core_send.at[h], recv_sem=core_recv.at[h],
            device_id={"tp": core_peer}, device_id_type=MESH,
        )

    def y_copy():
        return pltpu.make_async_remote_copy(
            src_ref=sum_core, dst_ref=recv_y, send_sem=y_send, recv_sem=y_recv,
            device_id={"tp": y_peer}, device_id_type=MESH,
        )

    far = core_copy(1 - high)
    near = core_copy(high)
    far.start()
    near.start()
    far.wait_recv()
    sum_core[...] = part[2 * (1 - high) + low] + recv_core[1 - high]
    across = y_copy()
    across.start()
    near.wait_recv()
    total[...] = part[2 * high + low] + recv_core[high]
    across.wait()
    total[...] += recv_y[...]

    def dom_copy(o):
        peer = lax.rem(d + o, doms)
        return pltpu.make_async_remote_copy(
            src_ref=total.at[pl.ds(pl.multiple_of(peer * rows, 8), rows)], dst_ref=recv_dom.at[o],
            send_sem=dom_send.at[o], recv_sem=dom_recv.at[o],
            device_id={"dom": peer}, device_id_type=MESH,
        )

    def small_copy(o):
        peer = lax.rem(d + o, doms)
        return pltpu.make_async_remote_copy(
            src_ref=total.at[pl.ds(width, 8)], dst_ref=recv_small.at[d],
            send_sem=small_send.at[o], recv_sem=small_recv.at[o],
            device_id={"dom": peer}, device_id_type=MESH,
        )

    @pl.loop(1, doms)
    def _(o):
        dom_copy(o).start()

    @pl.loop(1, doms)
    def _(o):
        small_copy(o).start()

    mine = pl.ds(pl.multiple_of(d * rows, 8), rows)
    full[mine, :] = total[mine, :]
    recv_small[d] = total[pl.ds(width, 8), :]

    @pl.loop(1, doms)
    def _(o):
        dom_copy(o).wait()
        full[mine, :] += recv_dom[o]

    def full_copy(o):
        return pltpu.make_async_remote_copy(
            src_ref=full.at[mine], dst_ref=full.at[mine],
            send_sem=full_send.at[o], recv_sem=full_recv.at[o],
            device_id={"dom": lax.rem(d + o, doms)}, device_id_type=MESH,
        )

    @pl.loop(1, doms)
    def _(o):
        full_copy(o).start()

    @pl.loop(1, doms)
    def _(o):
        small_copy(o).wait()

    small = recv_small[0]
    for k in range(1, doms):
        small += recv_small[k]
    small_out[...] = small

    @pl.loop(1, doms)
    def _(o):
        full_copy(o).wait()

    far.wait_send()
    near.wait_send()
    weight_out[...] = full[...]


def reduce_all(doms, lanes, first, second, back, stack, agg, slope, gain):
    own_count, block, width = first.shape
    wanted = back.shape[0]
    quarter = width // lanes
    tall = width + 8
    rows = width // doms
    dma = pltpu.SemaphoreType.DMA
    return pl.pallas_call(
        functools.partial(reduce_kernel, doms, own_count, wanted),
        in_specs=[vmem()] * 7,
        out_specs=[vmem()] * 2,
        out_shape=(
            jax.ShapeDtypeStruct((width, quarter), jnp.float32),
            jax.ShapeDtypeStruct((8, quarter), jnp.float32),
        ),
        scratch_shapes=[
            pltpu.VMEM((lanes, tall, quarter), jnp.float32),
            pltpu.VMEM((wanted, block, width), jnp.bfloat16),
            pltpu.VMEM(((own_count + wanted) * block, width), jnp.bfloat16),
            pltpu.VMEM((2, tall, quarter), jnp.float32),
            pltpu.VMEM((tall, quarter), jnp.float32),
            pltpu.VMEM((tall, quarter), jnp.float32),
            pltpu.VMEM((tall, quarter), jnp.float32),
            pltpu.VMEM((doms, rows, quarter), jnp.float32),
            pltpu.VMEM((doms, 8, quarter), jnp.float32),
            pltpu.VMEM((width, quarter), jnp.float32),
            dma((2,)), dma((2,)), dma, dma,
            dma((doms,)), dma((doms,)), dma((doms,)), dma((doms,)), dma((doms,)), dma((doms,)),
            dma((wanted,)), dma((wanted,)),
        ],
        compiler_params=pltpu.CompilerParams(
            collective_id=1, has_side_effects=True, vmem_limit_bytes=VMEM_LIMIT
        ),
    )(first, second, back, stack, agg, slope, gain)


def body(
    features, adjacency, node_mask, mask_token, enc_weight, enc_bias, gain, requests,
    pair_first, pair_second, label_words, pair_count,
):
    nodes, width = features.shape
    block = adjacency.shape[1]
    nblocks = nodes // block
    doms = lax.axis_size("dom")
    lanes = lax.axis_size("tp")
    own_count = nblocks // lanes
    wanted = doms // lanes
    gain_row = gain.reshape(1, width)
    stack, scaled, agg, slope = front(
        own_count, wanted, requests.reshape(doms),
        features.reshape(nblocks, block, width),
        adjacency.reshape(nblocks, block, block),
        node_mask.reshape(nblocks, 1, block),
        mask_token.reshape(1, width), enc_weight, enc_bias.reshape(1, -1), gain_row,
    )
    first, second, back = decode(
        pair_first[0, 0], pair_second[0, 0], pair_count.reshape(1), label_words[0, 0], stack, scaled
    )
    weight_grad, small = reduce_all(doms, lanes, first, second, back, stack, agg, slope, gain_row)
    return weight_grad, small[0], small[1]


def solution(mesh):
    placed = (
        P("dom", None),
        P("dom", None),
        P("dom"),
        P(),
        P(None, "tp"),
        P("tp"),
        P(),
        P(None, "dom"),
        P("dom", "tp", None),
        P("dom", "tp", None),
        P("dom", "tp", None, None, None),
        P("dom", "tp"),
    )
    return jax.shard_map(
        body,
        mesh=mesh,
        in_specs=placed,
        out_specs=(P(None, "tp"), P("tp"), P("tp")),
        check_vma=False,
    )
```

```python
import functools

import jax
import jax.numpy as jnp
from jax import lax
from jax.experimental import pallas as pl
from jax.experimental.pallas import tpu as pltpu
from jax.sharding import PartitionSpec as P

UNROLL = 4
INV_NORM = 1.0 / 256.0
MESH = pl.DeviceIdType.MESH
VMEM_LIMIT = 32 * 1024 * 1024
FRONT_LIMIT = 60 * 1024 * 1024


def sigmoid(value):
    return 0.5 * jnp.tanh(0.5 * value) + 0.5


def served(lane):
    return lax.rem(lane, 2) * 2 + lax.div(lane, 2)


def vmem():
    return pl.BlockSpec(memory_space=pltpu.VMEM)


def smem():
    return pl.BlockSpec(memory_space=pltpu.SMEM)


def front_kernel(
    own_count, wanted, requests, feat_hbm, adj_hbm, mask_hbm, token_hbm, weight_hbm, bias_hbm, gain_hbm,
    stack_out, scaled_out, agg_out, slope_out,
    feat, adj, mask, token, bias, gain, gathered, packed, asked, landed,
    feat_sem, w_send, w_recv, z_send, z_recv,
):
    d = lax.axis_index("dom")
    t = lax.axis_index("tp")
    low = lax.rem(t, 2)
    high = lax.div(t, 2)
    core_peer = high * 2 + (1 - low)
    y_peer = (1 - high) * 2 + low
    a = lax.div(d, wanted)
    j = lax.rem(d, wanted)
    width, quarter = weight_hbm.shape
    block = mask.shape[2]

    fetches = [
        pltpu.make_async_copy(source, target, feat_sem.at[k])
        for k, (source, target) in enumerate(
            (
                (weight_hbm, packed.at[pl.ds(0, width)]),
                (bias_hbm, bias),
                (token_hbm, token),
                (mask_hbm, mask),
                (adj_hbm, adj),
                (feat_hbm, feat),
                (gain_hbm, gain),
            )
        )
    ]
    for fetch in fetches:
        fetch.start()

    barrier = pltpu.get_barrier_semaphore()
    for peer in (core_peer, y_peer):
        pl.semaphore_signal(barrier, inc=1, device_id={"tp": peer}, device_id_type=MESH)

    def pair_of(c):
        return served(t) * wanted + lax.rem(j + c, wanted), a

    alone = jnp.logical_and(a == t, served(t) == t)
    for c in range(wanted):
        target = pair_of(c)
        source = t * wanted + lax.rem(j - c + wanted, wanted), served(a)

        def greet():
            pl.semaphore_signal(barrier, inc=1, device_id=target, device_id_type=MESH)
            pl.semaphore_signal(barrier, inc=1, device_id=source, device_id_type=MESH)

        if c == 0:
            pl.when(jnp.logical_not(alone))(greet)
        else:
            greet()

    columns = lambda c: pl.ds(pl.multiple_of(c * quarter, quarter), quarter)
    fetches[0].wait()
    fetches[1].wait()
    packed[pl.ds(width, 16), :] = jnp.broadcast_to(bias[...], (16, quarter))
    gathered[:, columns(t)] = packed[...]
    pl.semaphore_wait(barrier, 2 + 2 * wanted - jnp.where(alone, 2, 0))

    def weight_copy(k, source, column, peer):
        return pltpu.make_async_remote_copy(
            src_ref=source, dst_ref=gathered.at[:, columns(column)],
            send_sem=w_send.at[k], recv_sem=w_recv.at[k],
            device_id={"tp": peer}, device_id_type=MESH,
        )

    across = weight_copy(0, packed, t, y_peer)
    near = weight_copy(1, packed, t, core_peer)
    relay = weight_copy(2, gathered.at[:, columns(y_peer)], y_peer, core_peer)
    across.start()
    near.start()

    rows = lax.broadcasted_iota(jnp.int32, (block, block), 0)
    cols = lax.broadcasted_iota(jnp.int32, (block, block), 1)
    for fetch in fetches[2:]:
        fetch.wait()
    token32 = token[...].astype(jnp.float32)

    def aggregate(node_block, spot):
        hidden = jnp.sum(
            jnp.where(rows == cols, mask[node_block].astype(jnp.float32), 0.0), axis=1, keepdims=True
        )
        masked32 = jnp.where(hidden == 1.0, token32, feat[node_block].astype(jnp.float32))
        mixed = jnp.dot(
            adj[node_block], masked32.astype(jnp.bfloat16), preferred_element_type=jnp.float32
        )
        agg_out[spot] = (masked32 + mixed).astype(jnp.bfloat16)

    for k in range(wanted):
        aggregate(requests[served(t) * wanted + k], own_count + k)
    across.wait_recv()
    relay.start()
    for k in range(own_count):
        aggregate(t * own_count + k, k)
    near.wait_recv()
    relay.wait_recv()

    matrix = gathered[:width, :]
    shift = gathered[width : width + 1, :].astype(jnp.float32)

    def activate(spot, many):
        agg = agg_out[pl.ds(spot, many)].reshape(many * block, width)
        pre = jnp.dot(agg, matrix, preferred_element_type=jnp.float32) + shift
        sig = sigmoid(pre)
        slope_out[pl.ds(spot, many)] = (sig * (1.0 + pre * (1.0 - sig))).reshape(many, block, width)
        return (pre * sig).astype(jnp.bfloat16).reshape(many, block, width)

    for k in range(wanted):
        asked[k] = activate(own_count + k, 1)[0]

    def z_copy(c):
        return pltpu.make_async_remote_copy(
            src_ref=asked.at[lax.rem(j + c, wanted)], dst_ref=landed.at[j],
            send_sem=z_send.at[c], recv_sem=z_recv.at[c],
            device_id=pair_of(c), device_id_type=MESH,
        )

    pl.when(jnp.logical_not(alone))(lambda: z_copy(0).start())
    for c in range(1, wanted):
        z_copy(c).start()

    @pl.when(alone)
    def _():
        landed[j] = asked[j]

    for k in range(0, own_count, 2):
        z = activate(k, 2)
        stack_out[pl.ds(k, 2)] = z
        scaled_out[pl.ds(k, 2)] = (z.astype(jnp.float32) * gain[...][None]).astype(jnp.bfloat16)

    pl.when(jnp.logical_not(alone))(lambda: z_copy(0).wait())
    for c in range(1, wanted):
        z_copy(c).wait()
    for k in range(wanted):
        stack_out[own_count + k] = landed[k]
    across.wait_send()
    near.wait_send()
    relay.wait_send()


def front(own_count, wanted, requests, feat, adj, mask, token, weight, bias, gain):
    nblocks, block, width = feat.shape
    quarter = weight.shape[1]
    total = own_count + wanted
    dma = pltpu.SemaphoreType.DMA
    anywhere = pl.BlockSpec(memory_space=pltpu.HBM)
    return pl.pallas_call(
        functools.partial(front_kernel, own_count, wanted),
        in_specs=[smem()] + [anywhere] * 7,
        out_specs=[vmem()] * 4,
        out_shape=(
            jax.ShapeDtypeStruct((total, block, width), jnp.bfloat16),
            jax.ShapeDtypeStruct((own_count, block, width), jnp.bfloat16),
            jax.ShapeDtypeStruct((total, block, width), jnp.bfloat16),
            jax.ShapeDtypeStruct((total, block, width), jnp.float32),
        ),
        scratch_shapes=[
            pltpu.VMEM((nblocks, block, width), jnp.bfloat16),
            pltpu.VMEM((nblocks, block, block), jnp.bfloat16),
            pltpu.VMEM((nblocks, 1, block), jnp.int32),
            pltpu.VMEM((1, width), jnp.bfloat16),
            pltpu.VMEM((1, quarter), jnp.bfloat16),
            pltpu.VMEM((1, width), jnp.float32),
            pltpu.VMEM((width + 16, width), jnp.bfloat16),
            pltpu.VMEM((width + 16, quarter), jnp.bfloat16),
            pltpu.VMEM((wanted, block, width), jnp.bfloat16),
            pltpu.VMEM((wanted, block, width), jnp.bfloat16),
            dma((7,)), dma((3,)), dma((3,)), dma((wanted,)), dma((wanted,)),
        ],
        compiler_params=pltpu.CompilerParams(
            collective_id=0, has_side_effects=True, vmem_limit_bytes=FRONT_LIMIT
        ),
    )(requests, feat, adj, mask, token, weight, bias, gain)


def run_pairs(first, second, count, words, stack, scaled, first_acc, second_acc):
    live_count = count[0]
    block = stack.shape[1]
    shifts = lax.broadcasted_iota(jnp.int32, (block // 16, 16, block), 1)

    @pl.loop(0, pl.cdiv(live_count, UNROLL))
    def _(step):
        results = []
        for k in range(UNROLL):
            spot = step * UNROLL + k
            live = spot < live_count
            slot = jnp.where(live, spot, 0)
            ia = first[slot]
            ib = second[slot]
            scaled_a = scaled[ia]
            tile_b = stack[ib]
            logits = lax.dot_general(
                scaled_a, tile_b, (((1,), (1,)), ((), ())), preferred_element_type=jnp.float32
            )
            bits = jnp.bitwise_and(jnp.right_shift(words[slot][:, None, :], shifts), 1)
            label = bits.reshape(block, block).astype(jnp.float32)
            factor = jnp.where(live, INV_NORM, 0.0)
            slope = ((sigmoid(logits) - label) * factor).astype(jnp.bfloat16)
            part_a = jnp.dot(slope, tile_b, preferred_element_type=jnp.float32)
            part_b = lax.dot_general(
                slope, scaled_a, (((0,), (0,)), ((), ())), preferred_element_type=jnp.float32
            )
            results.append((ia, ib, part_a, part_b))
        for ia, ib, part_a, part_b in results:
            first_acc[ia] += part_a
            second_acc[ib] += part_b


def decode_kernel(first, second, count, words, stack, scaled, first_acc, second_out, back_out, second_acc):
    own_count = scaled.shape[0]
    first_acc[...] = jnp.zeros_like(first_acc)
    second_acc[...] = jnp.zeros_like(second_acc)
    run_pairs(first, second, count, words, stack, scaled, first_acc, second_acc)
    second_out[...] = second_acc[:own_count]
    back_out[...] = second_acc[own_count:].astype(jnp.bfloat16)


def decode(first, second, count, words, stack, scaled):
    total, block, width = stack.shape
    own_count = scaled.shape[0]
    return pl.pallas_call(
        decode_kernel,
        in_specs=[smem()] * 3 + [vmem()] * 3,
        out_specs=[vmem()] * 3,
        out_shape=(
            jax.ShapeDtypeStruct((own_count, block, width), jnp.float32),
            jax.ShapeDtypeStruct((own_count, block, width), jnp.float32),
            jax.ShapeDtypeStruct((total - own_count, block, width), jnp.bfloat16),
        ),
        scratch_shapes=[pltpu.VMEM((total, block, width), jnp.float32)],
        compiler_params=pltpu.CompilerParams(vmem_limit_bytes=VMEM_LIMIT),
        cost_estimate=pl.CostEstimate(
            flops=64 * 6 * block * block * width, bytes_accessed=8 << 20, transcendentals=0
        ),
    )(first, second, count, words, stack, scaled)


def reduce_kernel(
    doms, own_count, wanted, first, second, back, stack, agg, slope, gain, weight_out, bias_out, gain_out,
    part, home, dpre, recv_core, sum_core, recv_y, total, recv_dom, recv_small, full,
    core_send, core_recv, y_send, y_recv, dom_send, dom_recv, small_send, small_recv,
    full_send, full_recv, home_send, home_recv,
):
    d = lax.axis_index("dom")
    t = lax.axis_index("tp")
    low = lax.rem(t, 2)
    high = lax.div(t, 2)
    core_peer = high * 2 + (1 - low)
    y_peer = (1 - high) * 2 + low
    width = full.shape[0]
    rows = width // doms

    barrier = pltpu.get_barrier_semaphore()
    for peer in (core_peer, y_peer):
        pl.semaphore_signal(barrier, inc=1, device_id={"tp": peer}, device_id_type=MESH)

    @pl.loop(1, doms)
    def _(o):
        pl.semaphore_signal(
            barrier, inc=1, device_id={"dom": lax.rem(d + o, doms)}, device_id_type=MESH
        )

    a = lax.div(d, wanted)
    j = lax.rem(d, wanted)

    def pair_of(c):
        return t * wanted + lax.rem(j - c + wanted, wanted), served(a)

    alone = jnp.logical_and(a == t, served(t) == t)
    for c in range(wanted):
        target = pair_of(c)
        source = served(t) * wanted + lax.rem(j + c, wanted), a

        def greet():
            pl.semaphore_signal(barrier, inc=1, device_id=target, device_id_type=MESH)
            pl.semaphore_signal(barrier, inc=1, device_id=source, device_id_type=MESH)

        if c == 0:
            pl.when(jnp.logical_not(alone))(greet)
        else:
            greet()

    pl.semaphore_wait(barrier, doms + 1 + 2 * wanted - jnp.where(alone, 2, 0))

    def home_copy(c):
        return pltpu.make_async_remote_copy(
            src_ref=back.at[lax.rem(j - c + wanted, wanted)], dst_ref=home.at[j],
            send_sem=home_send.at[c], recv_sem=home_recv.at[c],
            device_id=pair_of(c), device_id_type=MESH,
        )

    pl.when(jnp.logical_not(alone))(lambda: home_copy(0).start())
    for c in range(1, wanted):
        home_copy(c).start()

    @pl.when(alone)
    def _():
        home[j] = back[j]

    block = stack.shape[1]
    bias_sum = jnp.zeros((1, width), jnp.float32)
    gain_sum = jnp.zeros((1, width), jnp.float32)
    for k in range(own_count):
        value = first[k]
        gain_sum += jnp.sum(stack[k].astype(jnp.float32) * value, axis=0, keepdims=True)
        value = (gain[...] * value + second[k]) * slope[k]
        bias_sum += jnp.sum(value, axis=0, keepdims=True)
        dpre[pl.ds(k * block, block), :] = value.astype(jnp.bfloat16)

    lanes, _, quarter = part.shape

    def product(start, many, c):
        left = agg[pl.ds(start, many)].reshape(many * block, width)
        right = dpre[pl.ds(start * block, many * block), pl.ds(c * quarter, 2 * quarter)]
        return lax.dot_general(
            left, right, (((0,), (0,)), ((), ())), preferred_element_type=jnp.float32
        )

    for c in range(0, lanes, 2):
        both = product(0, own_count, c)
        for k in range(2):
            part[c + k, :width, :] = both[:, k * quarter : (k + 1) * quarter]

    pl.when(jnp.logical_not(alone))(lambda: home_copy(0).wait())
    for c in range(1, wanted):
        home_copy(c).wait()
    for k in range(wanted):
        value = home[k].astype(jnp.float32) * slope[own_count + k]
        bias_sum += jnp.sum(value, axis=0, keepdims=True)
        dpre[pl.ds((own_count + k) * block, block), :] = value.astype(jnp.bfloat16)
    for c in range(0, lanes, 2):
        both = product(own_count, wanted, c)
        for k in range(2):
            part[c + k, :width, :] += both[:, k * quarter : (k + 1) * quarter]
    row = lax.broadcasted_iota(jnp.int32, (8, width), 0)
    extra = jnp.where(row == 0, bias_sum, jnp.where(row == 1, gain_sum, 0.0))
    for c in range(lanes):
        part[c, pl.ds(width, 8), :] = extra[:, c * quarter : (c + 1) * quarter]

    def core_copy(h):
        return pltpu.make_async_remote_copy(
            src_ref=part.at[2 * h + 1 - low], dst_ref=recv_core.at[h],
            send_sem=core_send.at[h], recv_sem=core_recv.at[h],
            device_id={"tp": core_peer}, device_id_type=MESH,
        )

    def y_copy():
        return pltpu.make_async_remote_copy(
            src_ref=sum_core, dst_ref=recv_y, send_sem=y_send, recv_sem=y_recv,
            device_id={"tp": y_peer}, device_id_type=MESH,
        )

    far = core_copy(1 - high)
    near = core_copy(high)
    far.start()
    near.start()
    far.wait_recv()
    sum_core[...] = part[2 * (1 - high) + low] + recv_core[1 - high]
    across = y_copy()
    across.start()
    near.wait_recv()
    total[...] = part[2 * high + low] + recv_core[high]
    across.wait()
    total[...] += recv_y[...]

    def dom_copy(o):
        peer = lax.rem(d + o, doms)
        return pltpu.make_async_remote_copy(
            src_ref=total.at[pl.ds(pl.multiple_of(peer * rows, 8), rows)], dst_ref=recv_dom.at[o],
            send_sem=dom_send.at[o], recv_sem=dom_recv.at[o],
            device_id={"dom": peer}, device_id_type=MESH,
        )

    def small_copy(o):
        peer = lax.rem(d + o, doms)
        return pltpu.make_async_remote_copy(
            src_ref=total.at[pl.ds(width, 8)], dst_ref=recv_small.at[d],
            send_sem=small_send.at[o], recv_sem=small_recv.at[o],
            device_id={"dom": peer}, device_id_type=MESH,
        )

    @pl.loop(1, doms)
    def _(o):
        dom_copy(o).start()

    @pl.loop(1, doms)
    def _(o):
        small_copy(o).start()

    mine = pl.ds(pl.multiple_of(d * rows, 8), rows)
    full[mine, :] = total[mine, :]
    recv_small[d] = total[pl.ds(width, 8), :]

    @pl.loop(1, doms)
    def _(o):
        dom_copy(o).wait()
        full[mine, :] += recv_dom[o]

    def full_copy(o):
        return pltpu.make_async_remote_copy(
            src_ref=full.at[mine], dst_ref=full.at[mine],
            send_sem=full_send.at[o], recv_sem=full_recv.at[o],
            device_id={"dom": lax.rem(d + o, doms)}, device_id_type=MESH,
        )

    @pl.loop(1, doms)
    def _(o):
        full_copy(o).start()

    @pl.loop(1, doms)
    def _(o):
        small_copy(o).wait()

    small = recv_small[0]
    for k in range(1, doms):
        small += recv_small[k]
    bias_out[...] = small[0:1]
    gain_out[...] = small[1:2]

    @pl.loop(1, doms)
    def _(o):
        full_copy(o).wait()

    far.wait_send()
    near.wait_send()
    weight_out[...] = full[...]


def reduce_all(doms, lanes, first, second, back, stack, agg, slope, gain):
    own_count, block, width = first.shape
    wanted = back.shape[0]
    quarter = width // lanes
    tall = width + 8
    rows = width // doms
    dma = pltpu.SemaphoreType.DMA
    return pl.pallas_call(
        functools.partial(reduce_kernel, doms, own_count, wanted),
        in_specs=[vmem()] * 7,
        out_specs=[vmem()] * 3,
        out_shape=(
            jax.ShapeDtypeStruct((width, quarter), jnp.float32),
            jax.ShapeDtypeStruct((1, quarter), jnp.float32),
            jax.ShapeDtypeStruct((1, quarter), jnp.float32),
        ),
        scratch_shapes=[
            pltpu.VMEM((lanes, tall, quarter), jnp.float32),
            pltpu.VMEM((wanted, block, width), jnp.bfloat16),
            pltpu.VMEM(((own_count + wanted) * block, width), jnp.bfloat16),
            pltpu.VMEM((2, tall, quarter), jnp.float32),
            pltpu.VMEM((tall, quarter), jnp.float32),
            pltpu.VMEM((tall, quarter), jnp.float32),
            pltpu.VMEM((tall, quarter), jnp.float32),
            pltpu.VMEM((doms, rows, quarter), jnp.float32),
            pltpu.VMEM((doms, 8, quarter), jnp.float32),
            pltpu.VMEM((width, quarter), jnp.float32),
            dma((2,)), dma((2,)), dma, dma,
            dma((doms,)), dma((doms,)), dma((doms,)), dma((doms,)), dma((doms,)), dma((doms,)),
            dma((wanted,)), dma((wanted,)),
        ],
        compiler_params=pltpu.CompilerParams(
            collective_id=1, has_side_effects=True, vmem_limit_bytes=VMEM_LIMIT
        ),
    )(first, second, back, stack, agg, slope, gain)


def body(
    features, adjacency, node_mask, mask_token, enc_weight, enc_bias, gain, requests,
    pair_first, pair_second, label_words, pair_count,
):
    nodes, width = features.shape
    block = adjacency.shape[1]
    nblocks = nodes // block
    doms = lax.axis_size("dom")
    lanes = lax.axis_size("tp")
    own_count = nblocks // lanes
    wanted = doms // lanes
    gain_row = gain.reshape(1, width)
    stack, scaled, agg, slope = front(
        own_count, wanted, requests.reshape(doms),
        features.reshape(nblocks, block, width),
        adjacency.reshape(nblocks, block, block),
        node_mask.reshape(nblocks, 1, block),
        mask_token.reshape(1, width), enc_weight, enc_bias.reshape(1, -1), gain_row,
    )
    first, second, back = decode(
        pair_first[0, 0], pair_second[0, 0], pair_count.reshape(1), label_words[0, 0], stack, scaled
    )
    weight_grad, bias_grad, gain_grad = reduce_all(doms, lanes, first, second, back, stack, agg, slope, gain_row)
    return weight_grad, bias_grad.reshape(-1), gain_grad.reshape(-1)


def solution(mesh):
    placed = (
        P("dom", None),
        P("dom", None),
        P("dom"),
        P(),
        P(None, "tp"),
        P("tp"),
        P(),
        P(None, "dom"),
        P("dom", "tp", None),
        P("dom", "tp", None),
        P("dom", "tp", None, None, None),
        P("dom", "tp"),
    )
    return jax.shard_map(
        body,
        mesh=mesh,
        in_specs=placed,
        out_specs=(P(None, "tp"), P("tp"), P("tp")),
        check_vma=False,
    )
```

```python
import functools

import jax
import jax.numpy as jnp
from jax import lax
from jax.experimental import pallas as pl
from jax.experimental.pallas import tpu as pltpu
from jax.sharding import PartitionSpec as P

UNROLL = 4
INV_NORM = 1.0 / 256.0
MESH = pl.DeviceIdType.MESH
VMEM_LIMIT = 32 * 1024 * 1024
FRONT_LIMIT = 60 * 1024 * 1024


def sigmoid(value):
    return 0.5 * jnp.tanh(0.5 * value) + 0.5


def served(lane):
    return lax.rem(lane, 2) * 2 + lax.div(lane, 2)


def vmem():
    return pl.BlockSpec(memory_space=pltpu.VMEM)


def smem():
    return pl.BlockSpec(memory_space=pltpu.SMEM)


def front_kernel(
    own_count, wanted, requests, feat_hbm, adj_hbm, mask_hbm, token_hbm, weight_hbm, bias_hbm, gain_hbm,
    stack_out, scaled_out, agg_out, slope_out,
    feat, adj, mask, token, bias, gain, gathered, packed, asked, landed,
    feat_sem, w_send, w_recv, z_send, z_recv,
):
    d = lax.axis_index("dom")
    t = lax.axis_index("tp")
    low = lax.rem(t, 2)
    high = lax.div(t, 2)
    core_peer = high * 2 + (1 - low)
    y_peer = (1 - high) * 2 + low
    a = lax.div(d, wanted)
    j = lax.rem(d, wanted)
    width, quarter = weight_hbm.shape
    block = mask.shape[2]

    fetches = [
        pltpu.make_async_copy(source, target, feat_sem.at[k])
        for k, (source, target) in enumerate(
            (
                (weight_hbm, packed.at[pl.ds(0, width)]),
                (bias_hbm, bias),
                (token_hbm, token),
                (mask_hbm, mask),
                (adj_hbm, adj),
                (feat_hbm, feat),
                (gain_hbm, gain),
            )
        )
    ]
    for fetch in fetches:
        fetch.start()

    barrier = pltpu.get_barrier_semaphore()
    for peer in (core_peer, y_peer):
        pl.semaphore_signal(barrier, inc=1, device_id={"tp": peer}, device_id_type=MESH)

    def pair_of(c):
        return served(t) * wanted + lax.rem(j + c, wanted), a

    alone = jnp.logical_and(a == t, served(t) == t)
    for c in range(wanted):
        target = pair_of(c)
        source = t * wanted + lax.rem(j - c + wanted, wanted), served(a)

        def greet():
            pl.semaphore_signal(barrier, inc=1, device_id=target, device_id_type=MESH)
            pl.semaphore_signal(barrier, inc=1, device_id=source, device_id_type=MESH)

        if c == 0:
            pl.when(jnp.logical_not(alone))(greet)
        else:
            greet()

    columns = lambda c: pl.ds(pl.multiple_of(c * quarter, quarter), quarter)
    fetches[0].wait()
    fetches[1].wait()
    packed[pl.ds(width, 16), :] = jnp.broadcast_to(bias[...], (16, quarter))
    gathered[:, columns(t)] = packed[...]
    pl.semaphore_wait(barrier, 2 + 2 * wanted - jnp.where(alone, 2, 0))

    def weight_copy(k, source, column, peer):
        return pltpu.make_async_remote_copy(
            src_ref=source, dst_ref=gathered.at[:, columns(column)],
            send_sem=w_send.at[k], recv_sem=w_recv.at[k],
            device_id={"tp": peer}, device_id_type=MESH,
        )

    across = weight_copy(0, packed, t, y_peer)
    near = weight_copy(1, packed, t, core_peer)
    relay = weight_copy(2, gathered.at[:, columns(y_peer)], y_peer, core_peer)
    across.start()
    near.start()

    rows = lax.broadcasted_iota(jnp.int32, (block, block), 0)
    cols = lax.broadcasted_iota(jnp.int32, (block, block), 1)
    for fetch in fetches[2:]:
        fetch.wait()
    token32 = token[...].astype(jnp.float32)

    def aggregate(node_block):
        hidden = jnp.sum(
            jnp.where(rows == cols, mask[node_block].astype(jnp.float32), 0.0), axis=1, keepdims=True
        )
        masked32 = jnp.where(hidden == 1.0, token32, feat[node_block].astype(jnp.float32))
        mixed = jnp.dot(
            adj[node_block], masked32.astype(jnp.bfloat16), preferred_element_type=jnp.float32
        )
        return (masked32 + mixed).astype(jnp.bfloat16)

    for k in range(wanted):
        asked[k] = aggregate(requests[served(t) * wanted + k])

    def agg_copy(c):
        return pltpu.make_async_remote_copy(
            src_ref=asked.at[lax.rem(j + c, wanted)], dst_ref=landed.at[j],
            send_sem=z_send.at[c], recv_sem=z_recv.at[c],
            device_id=pair_of(c), device_id_type=MESH,
        )

    pl.when(jnp.logical_not(alone))(lambda: agg_copy(0).start())
    for c in range(1, wanted):
        agg_copy(c).start()

    @pl.when(alone)
    def _():
        landed[j] = asked[j]

    across.wait_recv()
    relay.start()
    for k in range(own_count):
        agg_out[k] = aggregate(t * own_count + k)
    near.wait_recv()
    relay.wait_recv()

    matrix = gathered[:width, :]
    shift = gathered[width : width + 1, :].astype(jnp.float32)

    def activate(spot, many):
        agg = agg_out[pl.ds(spot, many)].reshape(many * block, width)
        pre = jnp.dot(agg, matrix, preferred_element_type=jnp.float32) + shift
        sig = sigmoid(pre)
        slope_out[pl.ds(spot, many)] = (sig * (1.0 + pre * (1.0 - sig))).reshape(many, block, width)
        z = (pre * sig).astype(jnp.bfloat16).reshape(many, block, width)
        stack_out[pl.ds(spot, many)] = z
        return z

    for k in range(0, own_count, 2):
        z = activate(k, 2)
        scaled_out[pl.ds(k, 2)] = (z.astype(jnp.float32) * gain[...][None]).astype(jnp.bfloat16)

    pl.when(jnp.logical_not(alone))(lambda: agg_copy(0).wait())
    for c in range(1, wanted):
        agg_copy(c).wait()
    for k in range(0, wanted, 2):
        agg_out[pl.ds(own_count + k, 2)] = landed[pl.ds(k, 2)]
        activate(own_count + k, 2)
    across.wait_send()
    near.wait_send()
    relay.wait_send()


def front(own_count, wanted, requests, feat, adj, mask, token, weight, bias, gain):
    nblocks, block, width = feat.shape
    quarter = weight.shape[1]
    total = own_count + wanted
    dma = pltpu.SemaphoreType.DMA
    anywhere = pl.BlockSpec(memory_space=pltpu.HBM)
    return pl.pallas_call(
        functools.partial(front_kernel, own_count, wanted),
        in_specs=[smem()] + [anywhere] * 7,
        out_specs=[vmem()] * 4,
        out_shape=(
            jax.ShapeDtypeStruct((total, block, width), jnp.bfloat16),
            jax.ShapeDtypeStruct((own_count, block, width), jnp.bfloat16),
            jax.ShapeDtypeStruct((total, block, width), jnp.bfloat16),
            jax.ShapeDtypeStruct((total, block, width), jnp.float32),
        ),
        scratch_shapes=[
            pltpu.VMEM((nblocks, block, width), jnp.bfloat16),
            pltpu.VMEM((nblocks, block, block), jnp.bfloat16),
            pltpu.VMEM((nblocks, 1, block), jnp.int32),
            pltpu.VMEM((1, width), jnp.bfloat16),
            pltpu.VMEM((1, quarter), jnp.bfloat16),
            pltpu.VMEM((1, width), jnp.float32),
            pltpu.VMEM((width + 16, width), jnp.bfloat16),
            pltpu.VMEM((width + 16, quarter), jnp.bfloat16),
            pltpu.VMEM((wanted, block, width), jnp.bfloat16),
            pltpu.VMEM((wanted, block, width), jnp.bfloat16),
            dma((7,)), dma((3,)), dma((3,)), dma((wanted,)), dma((wanted,)),
        ],
        compiler_params=pltpu.CompilerParams(
            collective_id=0, has_side_effects=True, vmem_limit_bytes=FRONT_LIMIT
        ),
    )(requests, feat, adj, mask, token, weight, bias, gain)


def run_pairs(first, second, count, words, stack, scaled, first_acc, second_acc):
    live_count = count[0]
    block = stack.shape[1]
    shifts = lax.broadcasted_iota(jnp.int32, (block // 16, 16, block), 1)

    @pl.loop(0, pl.cdiv(live_count, UNROLL))
    def _(step):
        results = []
        for k in range(UNROLL):
            spot = step * UNROLL + k
            live = spot < live_count
            slot = jnp.where(live, spot, 0)
            ia = first[slot]
            ib = second[slot]
            scaled_a = scaled[ia]
            tile_b = stack[ib]
            logits = lax.dot_general(
                scaled_a, tile_b, (((1,), (1,)), ((), ())), preferred_element_type=jnp.float32
            )
            bits = jnp.bitwise_and(jnp.right_shift(words[slot][:, None, :], shifts), 1)
            label = bits.reshape(block, block).astype(jnp.float32)
            factor = jnp.where(live, INV_NORM, 0.0)
            slope = ((sigmoid(logits) - label) * factor).astype(jnp.bfloat16)
            part_a = jnp.dot(slope, tile_b, preferred_element_type=jnp.float32)
            part_b = lax.dot_general(
                slope, scaled_a, (((0,), (0,)), ((), ())), preferred_element_type=jnp.float32
            )
            results.append((ia, ib, part_a, part_b))
        for ia, ib, part_a, part_b in results:
            first_acc[ia] += part_a
            second_acc[ib] += part_b


def decode_kernel(first, second, count, words, stack, scaled, first_acc, second_acc):
    first_acc[...] = jnp.zeros_like(first_acc)
    second_acc[...] = jnp.zeros_like(second_acc)
    run_pairs(first, second, count, words, stack, scaled, first_acc, second_acc)


def decode(first, second, count, words, stack, scaled):
    total, block, width = stack.shape
    own_count = scaled.shape[0]
    return pl.pallas_call(
        decode_kernel,
        in_specs=[smem()] * 3 + [vmem()] * 3,
        out_specs=[vmem()] * 2,
        out_shape=(
            jax.ShapeDtypeStruct((own_count, block, width), jnp.float32),
            jax.ShapeDtypeStruct((total, block, width), jnp.float32),
        ),
        compiler_params=pltpu.CompilerParams(vmem_limit_bytes=VMEM_LIMIT),
        cost_estimate=pl.CostEstimate(
            flops=64 * 6 * block * block * width, bytes_accessed=8 << 20, transcendentals=0
        ),
    )(first, second, count, words, stack, scaled)


def reduce_kernel(
    doms, own_count, total_count, first, second, stack, agg, slope, gain, weight_out, bias_out, gain_out,
    part, dpre, recv_core, sum_core, recv_y, total, recv_dom, recv_small, full,
    core_send, core_recv, y_send, y_recv, dom_send, dom_recv, small_send, small_recv,
    full_send, full_recv,
):
    d = lax.axis_index("dom")
    t = lax.axis_index("tp")
    low = lax.rem(t, 2)
    high = lax.div(t, 2)
    core_peer = high * 2 + (1 - low)
    y_peer = (1 - high) * 2 + low
    width = full.shape[0]
    rows = width // doms

    barrier = pltpu.get_barrier_semaphore()
    for peer in (core_peer, y_peer):
        pl.semaphore_signal(barrier, inc=1, device_id={"tp": peer}, device_id_type=MESH)

    @pl.loop(1, doms)
    def _(o):
        pl.semaphore_signal(
            barrier, inc=1, device_id={"dom": lax.rem(d + o, doms)}, device_id_type=MESH
        )

    block = stack.shape[1]
    bias_sum = jnp.zeros((1, width), jnp.float32)
    gain_sum = jnp.zeros((1, width), jnp.float32)
    for k in range(own_count):
        value = first[k]
        gain_sum += jnp.sum(stack[k].astype(jnp.float32) * value, axis=0, keepdims=True)
        value = (gain[...] * value + second[k]) * slope[k]
        bias_sum += jnp.sum(value, axis=0, keepdims=True)
        dpre[pl.ds(k * block, block), :] = value.astype(jnp.bfloat16)
    for k in range(own_count, total_count):
        value = second[k] * slope[k]
        bias_sum += jnp.sum(value, axis=0, keepdims=True)
        dpre[pl.ds(k * block, block), :] = value.astype(jnp.bfloat16)

    lanes, _, quarter = part.shape
    left = agg[...].reshape(total_count * block, width)
    row = lax.broadcasted_iota(jnp.int32, (8, width), 0)
    extra = jnp.where(row == 0, bias_sum, jnp.where(row == 1, gain_sum, 0.0))
    for c in range(0, lanes, 2):
        both = lax.dot_general(
            left, dpre[:, pl.ds(c * quarter, 2 * quarter)], (((0,), (0,)), ((), ())),
            preferred_element_type=jnp.float32,
        )
        for k in range(2):
            part[c + k, :width, :] = both[:, k * quarter : (k + 1) * quarter]
    for c in range(lanes):
        part[c, pl.ds(width, 8), :] = extra[:, c * quarter : (c + 1) * quarter]
    pl.semaphore_wait(barrier, doms + 1)

    def core_copy(h):
        return pltpu.make_async_remote_copy(
            src_ref=part.at[2 * h + 1 - low], dst_ref=recv_core.at[h],
            send_sem=core_send.at[h], recv_sem=core_recv.at[h],
            device_id={"tp": core_peer}, device_id_type=MESH,
        )

    def y_copy():
        return pltpu.make_async_remote_copy(
            src_ref=sum_core, dst_ref=recv_y, send_sem=y_send, recv_sem=y_recv,
            device_id={"tp": y_peer}, device_id_type=MESH,
        )

    far = core_copy(1 - high)
    near = core_copy(high)
    far.start()
    near.start()
    far.wait_recv()
    sum_core[...] = part[2 * (1 - high) + low] + recv_core[1 - high]
    across = y_copy()
    across.start()
    near.wait_recv()
    total[...] = part[2 * high + low] + recv_core[high]
    across.wait()
    total[...] += recv_y[...]

    def dom_copy(o):
        peer = lax.rem(d + o, doms)
        return pltpu.make_async_remote_copy(
            src_ref=total.at[pl.ds(pl.multiple_of(peer * rows, 8), rows)], dst_ref=recv_dom.at[o],
            send_sem=dom_send.at[o], recv_sem=dom_recv.at[o],
            device_id={"dom": peer}, device_id_type=MESH,
        )

    def small_copy(o):
        peer = lax.rem(d + o, doms)
        return pltpu.make_async_remote_copy(
            src_ref=total.at[pl.ds(width, 8)], dst_ref=recv_small.at[d],
            send_sem=small_send.at[o], recv_sem=small_recv.at[o],
            device_id={"dom": peer}, device_id_type=MESH,
        )

    @pl.loop(1, doms)
    def _(o):
        dom_copy(o).start()

    @pl.loop(1, doms)
    def _(o):
        small_copy(o).start()

    mine = pl.ds(pl.multiple_of(d * rows, 8), rows)
    full[mine, :] = total[mine, :]
    recv_small[d] = total[pl.ds(width, 8), :]

    @pl.loop(1, doms)
    def _(o):
        dom_copy(o).wait()
        full[mine, :] += recv_dom[o]

    def full_copy(o):
        return pltpu.make_async_remote_copy(
            src_ref=full.at[mine], dst_ref=full.at[mine],
            send_sem=full_send.at[o], recv_sem=full_recv.at[o],
            device_id={"dom": lax.rem(d + o, doms)}, device_id_type=MESH,
        )

    @pl.loop(1, doms)
    def _(o):
        full_copy(o).start()

    @pl.loop(1, doms)
    def _(o):
        small_copy(o).wait()

    small = recv_small[0]
    for k in range(1, doms):
        small += recv_small[k]
    bias_out[...] = small[0:1]
    gain_out[...] = small[1:2]

    @pl.loop(1, doms)
    def _(o):
        full_copy(o).wait()

    far.wait_send()
    near.wait_send()
    weight_out[...] = full[...]


def reduce_all(doms, lanes, first, second, stack, agg, slope, gain):
    own_count, block, width = first.shape
    total_count = second.shape[0]
    quarter = width // lanes
    tall = width + 8
    rows = width // doms
    dma = pltpu.SemaphoreType.DMA
    return pl.pallas_call(
        functools.partial(reduce_kernel, doms, own_count, total_count),
        in_specs=[vmem()] * 6,
        out_specs=[vmem()] * 3,
        out_shape=(
            jax.ShapeDtypeStruct((width, quarter), jnp.float32),
            jax.ShapeDtypeStruct((1, quarter), jnp.float32),
            jax.ShapeDtypeStruct((1, quarter), jnp.float32),
        ),
        scratch_shapes=[
            pltpu.VMEM((lanes, tall, quarter), jnp.float32),
            pltpu.VMEM((total_count * block, width), jnp.bfloat16),
            pltpu.VMEM((2, tall, quarter), jnp.float32),
            pltpu.VMEM((tall, quarter), jnp.float32),
            pltpu.VMEM((tall, quarter), jnp.float32),
            pltpu.VMEM((tall, quarter), jnp.float32),
            pltpu.VMEM((doms, rows, quarter), jnp.float32),
            pltpu.VMEM((doms, 8, quarter), jnp.float32),
            pltpu.VMEM((width, quarter), jnp.float32),
            dma((2,)), dma((2,)), dma, dma,
            dma((doms,)), dma((doms,)), dma((doms,)), dma((doms,)), dma((doms,)), dma((doms,)),
        ],
        compiler_params=pltpu.CompilerParams(
            collective_id=1, has_side_effects=True, vmem_limit_bytes=VMEM_LIMIT
        ),
    )(first, second, stack, agg, slope, gain)


def body(
    features, adjacency, node_mask, mask_token, enc_weight, enc_bias, gain, requests,
    pair_first, pair_second, label_words, pair_count,
):
    nodes, width = features.shape
    block = adjacency.shape[1]
    nblocks = nodes // block
    doms = lax.axis_size("dom")
    lanes = lax.axis_size("tp")
    own_count = nblocks // lanes
    wanted = doms // lanes
    gain_row = gain.reshape(1, width)
    stack, scaled, agg, slope = front(
        own_count, wanted, requests.reshape(doms),
        features.reshape(nblocks, block, width),
        adjacency.reshape(nblocks, block, block),
        node_mask.reshape(nblocks, 1, block),
        mask_token.reshape(1, width), enc_weight, enc_bias.reshape(1, -1), gain_row,
    )
    first, second = decode(
        pair_first[0, 0], pair_second[0, 0], pair_count.reshape(1), label_words[0, 0], stack, scaled
    )
    weight_grad, bias_grad, gain_grad = reduce_all(doms, lanes, first, second, stack, agg, slope, gain_row)
    return weight_grad, bias_grad.reshape(-1), gain_grad.reshape(-1)


def solution(mesh):
    placed = (
        P("dom", None),
        P("dom", None),
        P("dom"),
        P(),
        P(None, "tp"),
        P("tp"),
        P(),
        P(None, "dom"),
        P("dom", "tp", None),
        P("dom", "tp", None),
        P("dom", "tp", None, None, None),
        P("dom", "tp"),
    )
    return jax.shard_map(
        body,
        mesh=mesh,
        in_specs=placed,
        out_specs=(P(None, "tp"), P("tp"), P("tp")),
        check_vma=False,
    )
```

```python
import functools

import jax
import jax.numpy as jnp
from jax import lax
from jax.experimental import pallas as pl
from jax.experimental.pallas import tpu as pltpu
from jax.sharding import PartitionSpec as P

UNROLL = 8
INV_NORM = 1.0 / 256.0
MESH = pl.DeviceIdType.MESH
VMEM_LIMIT = 32 * 1024 * 1024
FRONT_LIMIT = 60 * 1024 * 1024


def sigmoid(value):
    return 0.5 * jnp.tanh(0.5 * value) + 0.5


def served(lane):
    return lax.rem(lane, 2) * 2 + lax.div(lane, 2)


def vmem():
    return pl.BlockSpec(memory_space=pltpu.VMEM)


def smem():
    return pl.BlockSpec(memory_space=pltpu.SMEM)


def front_kernel(
    own_count, wanted, requests, feat_hbm, adj_hbm, mask_hbm, token_hbm, weight_hbm, bias_hbm, gain_hbm,
    stack_out, scaled_out, agg_out, slope_out,
    feat, adj, mask, token, bias, gain, gathered, packed, asked, landed,
    feat_sem, w_send, w_recv, z_send, z_recv,
):
    d = lax.axis_index("dom")
    t = lax.axis_index("tp")
    low = lax.rem(t, 2)
    high = lax.div(t, 2)
    core_peer = high * 2 + (1 - low)
    y_peer = (1 - high) * 2 + low
    a = lax.div(d, wanted)
    j = lax.rem(d, wanted)
    width, quarter = weight_hbm.shape
    block = mask.shape[2]

    fetches = [
        pltpu.make_async_copy(source, target, feat_sem.at[k])
        for k, (source, target) in enumerate(
            (
                (weight_hbm, packed.at[pl.ds(0, width)]),
                (bias_hbm, bias),
                (token_hbm, token),
                (mask_hbm, mask),
                (adj_hbm, adj),
                (feat_hbm, feat),
                (gain_hbm, gain),
            )
        )
    ]
    for fetch in fetches:
        fetch.start()

    barrier = pltpu.get_barrier_semaphore()
    for peer in (core_peer, y_peer):
        pl.semaphore_signal(barrier, inc=1, device_id={"tp": peer}, device_id_type=MESH)

    def pair_of(c):
        return served(t) * wanted + lax.rem(j + c, wanted), a

    alone = jnp.logical_and(a == t, served(t) == t)
    for c in range(wanted):
        target = pair_of(c)
        source = t * wanted + lax.rem(j - c + wanted, wanted), served(a)

        def greet():
            pl.semaphore_signal(barrier, inc=1, device_id=target, device_id_type=MESH)
            pl.semaphore_signal(barrier, inc=1, device_id=source, device_id_type=MESH)

        if c == 0:
            pl.when(jnp.logical_not(alone))(greet)
        else:
            greet()

    columns = lambda c: pl.ds(pl.multiple_of(c * quarter, quarter), quarter)
    fetches[0].wait()
    fetches[1].wait()
    packed[pl.ds(width, 16), :] = jnp.broadcast_to(bias[...], (16, quarter))
    gathered[:, columns(t)] = packed[...]
    pl.semaphore_wait(barrier, 2 + 2 * wanted - jnp.where(alone, 2, 0))

    def weight_copy(k, source, column, peer):
        return pltpu.make_async_remote_copy(
            src_ref=source, dst_ref=gathered.at[:, columns(column)],
            send_sem=w_send.at[k], recv_sem=w_recv.at[k],
            device_id={"tp": peer}, device_id_type=MESH,
        )

    across = weight_copy(0, packed, t, y_peer)
    near = weight_copy(1, packed, t, core_peer)
    relay = weight_copy(2, gathered.at[:, columns(y_peer)], y_peer, core_peer)
    across.start()
    near.start()

    rows = lax.broadcasted_iota(jnp.int32, (block, block), 0)
    cols = lax.broadcasted_iota(jnp.int32, (block, block), 1)
    for fetch in fetches[2:]:
        fetch.wait()
    token32 = token[...].astype(jnp.float32)

    def aggregate(node_block):
        hidden = jnp.sum(
            jnp.where(rows == cols, mask[node_block].astype(jnp.float32), 0.0), axis=1, keepdims=True
        )
        masked32 = jnp.where(hidden == 1.0, token32, feat[node_block].astype(jnp.float32))
        mixed = jnp.dot(
            adj[node_block], masked32.astype(jnp.bfloat16), preferred_element_type=jnp.float32
        )
        return (masked32 + mixed).astype(jnp.bfloat16)

    for k in range(wanted):
        asked[k] = aggregate(requests[served(t) * wanted + k])

    def agg_copy(c):
        return pltpu.make_async_remote_copy(
            src_ref=asked.at[lax.rem(j + c, wanted)], dst_ref=landed.at[j],
            send_sem=z_send.at[c], recv_sem=z_recv.at[c],
            device_id=pair_of(c), device_id_type=MESH,
        )

    pl.when(jnp.logical_not(alone))(lambda: agg_copy(0).start())
    for c in range(1, wanted):
        agg_copy(c).start()

    @pl.when(alone)
    def _():
        landed[j] = asked[j]

    across.wait_recv()
    relay.start()
    for k in range(own_count):
        agg_out[k] = aggregate(t * own_count + k)
    near.wait_recv()
    relay.wait_recv()

    matrix = gathered[:width, :]
    shift = gathered[width : width + 1, :].astype(jnp.float32)

    def activate(spot, many):
        agg = agg_out[pl.ds(spot, many)].reshape(many * block, width)
        pre = jnp.dot(agg, matrix, preferred_element_type=jnp.float32) + shift
        sig = sigmoid(pre)
        slope_out[pl.ds(spot, many)] = (sig * (1.0 + pre * (1.0 - sig))).reshape(many, block, width)
        z = (pre * sig).astype(jnp.bfloat16).reshape(many, block, width)
        stack_out[pl.ds(spot, many)] = z
        return z

    for k in range(0, own_count, 2):
        z = activate(k, 2)
        scaled_out[pl.ds(k, 2)] = (z.astype(jnp.float32) * gain[...][None]).astype(jnp.bfloat16)

    pl.when(jnp.logical_not(alone))(lambda: agg_copy(0).wait())
    for c in range(1, wanted):
        agg_copy(c).wait()
    for k in range(0, wanted, 2):
        agg_out[pl.ds(own_count + k, 2)] = landed[pl.ds(k, 2)]
        activate(own_count + k, 2)
    across.wait_send()
    near.wait_send()
    relay.wait_send()


def front(own_count, wanted, requests, feat, adj, mask, token, weight, bias, gain):
    nblocks, block, width = feat.shape
    quarter = weight.shape[1]
    total = own_count + wanted
    dma = pltpu.SemaphoreType.DMA
    anywhere = pl.BlockSpec(memory_space=pltpu.HBM)
    return pl.pallas_call(
        functools.partial(front_kernel, own_count, wanted),
        in_specs=[smem()] + [anywhere] * 7,
        out_specs=[vmem()] * 4,
        out_shape=(
            jax.ShapeDtypeStruct((total, block, width), jnp.bfloat16),
            jax.ShapeDtypeStruct((own_count, block, width), jnp.bfloat16),
            jax.ShapeDtypeStruct((total, block, width), jnp.bfloat16),
            jax.ShapeDtypeStruct((total, block, width), jnp.float32),
        ),
        scratch_shapes=[
            pltpu.VMEM((nblocks, block, width), jnp.bfloat16),
            pltpu.VMEM((nblocks, block, block), jnp.bfloat16),
            pltpu.VMEM((nblocks, 1, block), jnp.int32),
            pltpu.VMEM((1, width), jnp.bfloat16),
            pltpu.VMEM((1, quarter), jnp.bfloat16),
            pltpu.VMEM((1, width), jnp.float32),
            pltpu.VMEM((width + 16, width), jnp.bfloat16),
            pltpu.VMEM((width + 16, quarter), jnp.bfloat16),
            pltpu.VMEM((wanted, block, width), jnp.bfloat16),
            pltpu.VMEM((wanted, block, width), jnp.bfloat16),
            dma((7,)), dma((3,)), dma((3,)), dma((wanted,)), dma((wanted,)),
        ],
        compiler_params=pltpu.CompilerParams(
            collective_id=0, has_side_effects=True, vmem_limit_bytes=FRONT_LIMIT
        ),
    )(requests, feat, adj, mask, token, weight, bias, gain)


def run_pairs(first, second, count, words, stack, scaled, first_acc, second_acc):
    live_count = count[0]
    block = stack.shape[1]
    shifts = lax.broadcasted_iota(jnp.int32, (block // 16, 16, block), 1)

    @pl.loop(0, pl.cdiv(live_count, UNROLL))
    def _(step):
        results = []
        for k in range(UNROLL):
            spot = step * UNROLL + k
            live = spot < live_count
            slot = jnp.where(live, spot, 0)
            ia = first[slot]
            ib = second[slot]
            scaled_a = scaled[ia]
            tile_b = stack[ib]
            logits = lax.dot_general(
                scaled_a, tile_b, (((1,), (1,)), ((), ())), preferred_element_type=jnp.float32
            )
            bits = jnp.bitwise_and(jnp.right_shift(words[slot][:, None, :], shifts), 1)
            label = bits.reshape(block, block).astype(jnp.float32)
            factor = jnp.where(live, INV_NORM, 0.0)
            slope = ((sigmoid(logits) - label) * factor).astype(jnp.bfloat16)
            part_a = jnp.dot(slope, tile_b, preferred_element_type=jnp.float32)
            part_b = lax.dot_general(
                slope, scaled_a, (((0,), (0,)), ((), ())), preferred_element_type=jnp.float32
            )
            results.append((ia, ib, part_a, part_b))
        for ia, ib, part_a, part_b in results:
            first_acc[ia] += part_a
            second_acc[ib] += part_b


def decode_kernel(first, second, count, words, stack, scaled, first_acc, second_acc):
    first_acc[...] = jnp.zeros_like(first_acc)
    second_acc[...] = jnp.zeros_like(second_acc)
    run_pairs(first, second, count, words, stack, scaled, first_acc, second_acc)


def decode(first, second, count, words, stack, scaled):
    total, block, width = stack.shape
    own_count = scaled.shape[0]
    return pl.pallas_call(
        decode_kernel,
        in_specs=[smem()] * 3 + [vmem()] * 3,
        out_specs=[vmem()] * 2,
        out_shape=(
            jax.ShapeDtypeStruct((own_count, block, width), jnp.float32),
            jax.ShapeDtypeStruct((total, block, width), jnp.float32),
        ),
        compiler_params=pltpu.CompilerParams(vmem_limit_bytes=VMEM_LIMIT),
        cost_estimate=pl.CostEstimate(
            flops=64 * 6 * block * block * width, bytes_accessed=8 << 20, transcendentals=0
        ),
    )(first, second, count, words, stack, scaled)


def reduce_kernel(
    doms, own_count, total_count, first, second, stack, agg, slope, gain, weight_out, bias_out, gain_out,
    part, dpre, recv_core, sum_core, recv_y, total, recv_dom, recv_small, full,
    core_send, core_recv, y_send, y_recv, dom_send, dom_recv, small_send, small_recv,
    full_send, full_recv,
):
    d = lax.axis_index("dom")
    t = lax.axis_index("tp")
    low = lax.rem(t, 2)
    high = lax.div(t, 2)
    core_peer = high * 2 + (1 - low)
    y_peer = (1 - high) * 2 + low
    width = full.shape[0]
    rows = width // doms

    barrier = pltpu.get_barrier_semaphore()
    for peer in (core_peer, y_peer):
        pl.semaphore_signal(barrier, inc=1, device_id={"tp": peer}, device_id_type=MESH)

    @pl.loop(1, doms)
    def _(o):
        pl.semaphore_signal(
            barrier, inc=1, device_id={"dom": lax.rem(d + o, doms)}, device_id_type=MESH
        )

    block = stack.shape[1]
    bias_sum = jnp.zeros((1, width), jnp.float32)
    gain_sum = jnp.zeros((1, width), jnp.float32)
    for k in range(own_count):
        value = first[k]
        gain_sum += jnp.sum(stack[k].astype(jnp.float32) * value, axis=0, keepdims=True)
        value = (gain[...] * value + second[k]) * slope[k]
        bias_sum += jnp.sum(value, axis=0, keepdims=True)
        dpre[pl.ds(k * block, block), :] = value.astype(jnp.bfloat16)
    for k in range(own_count, total_count):
        value = second[k] * slope[k]
        bias_sum += jnp.sum(value, axis=0, keepdims=True)
        dpre[pl.ds(k * block, block), :] = value.astype(jnp.bfloat16)

    lanes, _, quarter = part.shape
    left = agg[...].reshape(total_count * block, width)
    row = lax.broadcasted_iota(jnp.int32, (8, width), 0)
    extra = jnp.where(row == 0, bias_sum, jnp.where(row == 1, gain_sum, 0.0))
    for c in range(0, lanes, 2):
        both = lax.dot_general(
            left, dpre[:, pl.ds(c * quarter, 2 * quarter)], (((0,), (0,)), ((), ())),
            preferred_element_type=jnp.float32,
        )
        for k in range(2):
            part[c + k, :width, :] = both[:, k * quarter : (k + 1) * quarter]
    for c in range(lanes):
        part[c, pl.ds(width, 8), :] = extra[:, c * quarter : (c + 1) * quarter]
    pl.semaphore_wait(barrier, doms + 1)

    def core_copy(h):
        return pltpu.make_async_remote_copy(
            src_ref=part.at[2 * h + 1 - low], dst_ref=recv_core.at[h],
            send_sem=core_send.at[h], recv_sem=core_recv.at[h],
            device_id={"tp": core_peer}, device_id_type=MESH,
        )

    def y_copy():
        return pltpu.make_async_remote_copy(
            src_ref=sum_core, dst_ref=recv_y, send_sem=y_send, recv_sem=y_recv,
            device_id={"tp": y_peer}, device_id_type=MESH,
        )

    far = core_copy(1 - high)
    near = core_copy(high)
    far.start()
    near.start()
    far.wait_recv()
    sum_core[...] = part[2 * (1 - high) + low] + recv_core[1 - high]
    across = y_copy()
    across.start()
    near.wait_recv()
    total[...] = part[2 * high + low] + recv_core[high]
    across.wait()
    total[...] += recv_y[...]

    def dom_copy(o):
        peer = lax.rem(d + o, doms)
        return pltpu.make_async_remote_copy(
            src_ref=total.at[pl.ds(pl.multiple_of(peer * rows, 8), rows)], dst_ref=recv_dom.at[o],
            send_sem=dom_send.at[o], recv_sem=dom_recv.at[o],
            device_id={"dom": peer}, device_id_type=MESH,
        )

    def small_copy(o):
        peer = lax.rem(d + o, doms)
        return pltpu.make_async_remote_copy(
            src_ref=total.at[pl.ds(width, 8)], dst_ref=recv_small.at[d],
            send_sem=small_send.at[o], recv_sem=small_recv.at[o],
            device_id={"dom": peer}, device_id_type=MESH,
        )

    @pl.loop(1, doms)
    def _(o):
        dom_copy(o).start()

    @pl.loop(1, doms)
    def _(o):
        small_copy(o).start()

    mine = pl.ds(pl.multiple_of(d * rows, 8), rows)
    full[mine, :] = total[mine, :]
    recv_small[d] = total[pl.ds(width, 8), :]

    @pl.loop(1, doms)
    def _(o):
        dom_copy(o).wait()
        full[mine, :] += recv_dom[o]

    def full_copy(o):
        return pltpu.make_async_remote_copy(
            src_ref=full.at[mine], dst_ref=full.at[mine],
            send_sem=full_send.at[o], recv_sem=full_recv.at[o],
            device_id={"dom": lax.rem(d + o, doms)}, device_id_type=MESH,
        )

    @pl.loop(1, doms)
    def _(o):
        full_copy(o).start()

    @pl.loop(1, doms)
    def _(o):
        small_copy(o).wait()

    small = recv_small[0]
    for k in range(1, doms):
        small += recv_small[k]
    bias_out[...] = small[0:1]
    gain_out[...] = small[1:2]

    @pl.loop(1, doms)
    def _(o):
        full_copy(o).wait()

    far.wait_send()
    near.wait_send()
    weight_out[...] = full[...]


def reduce_all(doms, lanes, first, second, stack, agg, slope, gain):
    own_count, block, width = first.shape
    total_count = second.shape[0]
    quarter = width // lanes
    tall = width + 8
    rows = width // doms
    dma = pltpu.SemaphoreType.DMA
    return pl.pallas_call(
        functools.partial(reduce_kernel, doms, own_count, total_count),
        in_specs=[vmem()] * 6,
        out_specs=[vmem()] * 3,
        out_shape=(
            jax.ShapeDtypeStruct((width, quarter), jnp.float32),
            jax.ShapeDtypeStruct((1, quarter), jnp.float32),
            jax.ShapeDtypeStruct((1, quarter), jnp.float32),
        ),
        scratch_shapes=[
            pltpu.VMEM((lanes, tall, quarter), jnp.float32),
            pltpu.VMEM((total_count * block, width), jnp.bfloat16),
            pltpu.VMEM((2, tall, quarter), jnp.float32),
            pltpu.VMEM((tall, quarter), jnp.float32),
            pltpu.VMEM((tall, quarter), jnp.float32),
            pltpu.VMEM((tall, quarter), jnp.float32),
            pltpu.VMEM((doms, rows, quarter), jnp.float32),
            pltpu.VMEM((doms, 8, quarter), jnp.float32),
            pltpu.VMEM((width, quarter), jnp.float32),
            dma((2,)), dma((2,)), dma, dma,
            dma((doms,)), dma((doms,)), dma((doms,)), dma((doms,)), dma((doms,)), dma((doms,)),
        ],
        compiler_params=pltpu.CompilerParams(
            collective_id=1, has_side_effects=True, vmem_limit_bytes=VMEM_LIMIT
        ),
    )(first, second, stack, agg, slope, gain)


def body(
    features, adjacency, node_mask, mask_token, enc_weight, enc_bias, gain, requests,
    pair_first, pair_second, label_words, pair_count,
):
    nodes, width = features.shape
    block = adjacency.shape[1]
    nblocks = nodes // block
    doms = lax.axis_size("dom")
    lanes = lax.axis_size("tp")
    own_count = nblocks // lanes
    wanted = doms // lanes
    gain_row = gain.reshape(1, width)
    stack, scaled, agg, slope = front(
        own_count, wanted, requests.reshape(doms),
        features.reshape(nblocks, block, width),
        adjacency.reshape(nblocks, block, block),
        node_mask.reshape(nblocks, 1, block),
        mask_token.reshape(1, width), enc_weight, enc_bias.reshape(1, -1), gain_row,
    )
    first, second = decode(
        pair_first[0, 0], pair_second[0, 0], pair_count.reshape(1), label_words[0, 0], stack, scaled
    )
    weight_grad, bias_grad, gain_grad = reduce_all(doms, lanes, first, second, stack, agg, slope, gain_row)
    return weight_grad, bias_grad.reshape(-1), gain_grad.reshape(-1)


def solution(mesh):
    placed = (
        P("dom", None),
        P("dom", None),
        P("dom"),
        P(),
        P(None, "tp"),
        P("tp"),
        P(),
        P(None, "dom"),
        P("dom", "tp", None),
        P("dom", "tp", None),
        P("dom", "tp", None, None, None),
        P("dom", "tp"),
    )
    return jax.shard_map(
        body,
        mesh=mesh,
        in_specs=placed,
        out_specs=(P(None, "tp"), P("tp"), P("tp")),
        check_vma=False,
    )
```
